32 devices in a mesh: groups: 2 (over y), pert: 4 (over z), lat: 2 (over x), fld: 2 (over core).
Axes of the slice: x: 2, y: 2, z: 4, core: 2. Of those that a mesh axis runs over, the one named last changes fastest.
Arguments:
- perturb: float32 [64, 4, 32, 1024], P(('groups', 'pert', 'fld'), None, 'lat'), parts along dimension 0, may hold values from -6 to 6
- traj_store: float32 [8, 4, 32, 1024], P(('groups', 'pert'), 'fld', 'lat'), parts along dimension 0
- owners: int32 [6], P('groups'), parts along dimension 0, may hold values from 0 to 3, as said below
Outputs:
- advanced: float32 [64, 4, 32, 1024], P(('groups', 'pert', 'fld'), None, 'lat'), parts along dimension 0
The draws below stay inside these ranges and needn't reach their ends.
There are 2 independent parts, one for each index of `groups`. The reference program is written for one: setup_inputs(seed, part) draws one part's arguments, and reference() takes and returns one part's arrays. A program takes and returns all parts, laid end to end along the dimension named above; each array names one. Nothing has to cross between parts.
Inputs may be any that keep to these rules, and one draw needn't show every extreme that they name: `owners`: the 3 slots are distinct.
All inputs are finite; a program needn't handle non-finite values.
Results may differ from the reference program's by a relative error of at most 0.00002.
Values sent between devices are 32-bit elements; how exact they have to be, the bound alone decides.
A program may use at most 64 MiB of HBM per device.

```python
import jax
import jax.numpy as jnp
from jax import lax

NLON = 1024
FIELDS = 4
RECS = 3
STEPS = 6
LAT = 32
MEMBERS = 32
N_PERT = 4


def draw_traj_store(key, part):
    keys = jax.random.split(key, 4)
    shape = (N_PERT, LAT, NLON)
    wind_u = jax.random.uniform(keys[0], shape, jnp.float32, -1.0, 1.0)
    wind_v = jax.random.uniform(keys[1], shape, jnp.float32, -1.0, 1.0)
    depth = jax.random.uniform(keys[2], shape, jnp.float32, 0.5, 2.0)
    mixing = jnp.exp(jax.random.uniform(keys[3], shape, jnp.float32, jnp.log(0.3), jnp.log(1.2)))
    return jnp.stack([wind_u, wind_v, depth, mixing], axis=1).astype(jnp.float32)


def draw_owners(key, part):
    return jax.random.permutation(key, N_PERT)[:RECS].astype(jnp.int32)


def shard_levels(key, extent, pieces, least, top_value):
    level, own = 1.0, jax.random.fold_in(key, 6)
    for dim, blocks in pieces:
        steps = jnp.exp(jax.random.uniform(jax.random.fold_in(own, dim), (blocks,), jnp.float32, least / len(pieces), top_value / len(pieces)))
        level = level * jnp.repeat(steps, extent[dim] // blocks).reshape([-1 if axis == dim else 1 for axis in range(len(extent))])
    return level


def scatter_about(own_key, extent, scale, most, pieces=(), kind=jnp.bfloat16):
    array = scale * jax.random.normal(own_key, extent, jnp.float32)
    if pieces:
        array = array * shard_levels(own_key, extent, pieces, -0.22, 0.18)
    return jnp.clip(array, -most, most).astype(kind)


def setup_inputs(seed: int = 0, part: int = 0) -> dict:
    key_list = jax.random.split(jax.random.key(seed), 4)
    part_keys = jax.random.split(jax.random.fold_in(key_list[3], part), 4)
    perturb = scatter_about(part_keys[0], (MEMBERS, FIELDS, LAT, NLON), 1.0, 6.0, ((0, 8), (2, 2)), jnp.float32)
    traj_store = draw_traj_store(jax.random.fold_in(jax.random.fold_in(key_list[3], part), 71), part)
    owners = draw_owners(jax.random.fold_in(jax.random.fold_in(key_list[3], part), 71), part)
    return {"perturb": perturb, "traj_store": traj_store, "owners": owners}


time_step = 0.1
gravity = 1.0


def advance(padded, coef, coriolis):
    centre = padded[..., 1:-1, :]
    north = padded[..., 2:, :]
    south = padded[..., :-2, :]
    east = jnp.roll(centre, -1, axis=-1)
    west = jnp.roll(centre, 1, axis=-1)
    grad_x = (east - west) * 0.5
    grad_y = (north - south) * 0.5
    spread = east + west + north + south - 4.0 * centre
    tend = -(coef[0] * grad_x + coef[1] * grad_y) + coef[3] * spread
    diverge = grad_x[..., 1, :, :] + grad_y[..., 2, :, :]
    height = tend[..., 0, :, :] - coef[2] * diverge
    zonal = tend[..., 1, :, :] - gravity * grad_x[..., 0, :, :] + coriolis * centre[..., 2, :, :]
    merid = tend[..., 2, :, :] - gravity * grad_y[..., 0, :, :] - coriolis * centre[..., 1, :, :]
    tracer = tend[..., 3, :, :] - 0.5 * diverge
    return centre + time_step * jnp.stack([height, zonal, merid, tracer], axis=-3)


def interpolate(records, which):
    earlier = which // 3
    weight = (which % 3) / 3.0
    return (1.0 - weight) * records[earlier] + weight * records[earlier + 1]


def reference(perturb, traj_store, owners):
    records = jnp.take(traj_store, owners.astype(jnp.int32), axis=0)
    latrow = jnp.arange(LAT, dtype=jnp.int32).astype(jnp.float32)
    coriolis = jnp.sin(jnp.pi * ((latrow + 0.5) / LAT - 0.5))[:, None]
    coefs = [interpolate(records, which) for which in range(STEPS)]

    def member_run(member):
        state = member
        for which in range(STEPS):
            padded = jnp.pad(state, ((0, 0), (1, 1), (0, 0)))
            state = advance(padded, coefs[which], coriolis)
        return state

    return lax.map(member_run, perturb)
```

```python
import functools

import jax
import jax.numpy as jnp
import numpy as np
from jax import lax
from jax.experimental import pallas as pl
from jax.experimental.pallas import tpu as pltpu
from jax.sharding import PartitionSpec as P

STEPS = 6
MESH = pl.DeviceIdType.MESH
SUB = 8
CHUNKS = 4
CAPS = (1, 3, 5, 5)


def kernel(n, nlat, mem, rows, owners_ref, perturb_ref, traj_ref, out_ref,
           vin, tin, vout, state, rec, cor, own, *rest):
    gather = rest[:CHUNKS]
    (in_sem, out_sem, zsend, zrecv, csend, crecv, fsend, hsend, hrecv) = rest[CHUNKS:]
    z = lax.axis_index("pert")
    core = lax.axis_index("fld")
    lat = lax.axis_index("lat")
    other = 1 - core
    even = lat % 2 == 0
    near = jnp.where(even, lat + 1, lat - 1)
    far = jnp.where(even, lat - 1, lat + 1)
    has_near = near < nlat
    has_far = jnp.logical_and(far >= 0, far < nlat)
    span = rows // CHUNKS
    fields = 4
    mf = mem * fields
    wide = mf * SUB

    def phys(q):
        return jnp.where(even, rows - 1 - q, q)

    def line(s, r):
        return pl.multiple_of(((s * (rows + 2)) + r + 1) * wide, wide)

    def first_row(k):
        return jnp.where(even, rows - (k + 1) * span, k * span)

    t_in = pltpu.make_async_copy(traj_ref.at[0], tin, in_sem.at[0])
    t_in.start()
    s_in = pltpu.make_async_copy(perturb_ref, vin, in_sem.at[1])
    s_in.start()

    barrier = pltpu.get_barrier_semaphore()
    for t in range(n):
        @pl.when(z != t)
        def _():
            pl.semaphore_signal(barrier, inc=1, device_id={"pert": t}, device_id_type=MESH)
    pl.semaphore_signal(barrier, inc=1, device_id={"fld": other}, device_id_type=MESH)

    @pl.when(has_near)
    def _():
        pl.semaphore_signal(barrier, inc=1, device_id={"lat": near}, device_id_type=MESH)
    if nlat > 2:
        @pl.when(has_far)
        def _():
            pl.semaphore_signal(barrier, inc=1, device_id={"lat": far}, device_id_type=MESH)

    block = span * 2

    def piece(k, slot, half):
        return gather[k].at[pl.ds((slot * 2 + half) * block, block)]

    t_in.wait()
    halves = rows // SUB
    for f in range(2):
        for g in range(halves):
            for j in range(8):
                own[pl.ds((g * SUB * 2 + f) * SUB + j, SUB, stride=2 * SUB), :] = (
                    tin[f, g * SUB:(g + 1) * SUB, j * 128:(j + 1) * 128])
    for k in range(CHUNKS):
        for i in range(span * 2):
            at = (z * 2 + core) * block + i
            src = pl.multiple_of(first_row(k) * 2 * SUB, SUB) + i * SUB
            gather[k][at] = own[pl.ds(src, SUB), :]

    amount = n - 1 + 1 + jnp.where(has_near, 1, 0)
    if nlat > 2:
        amount = amount + jnp.where(has_far, 1, 0)
    pl.semaphore_wait(barrier, amount)

    def z_copy(k, target):
        own = piece(k, z, core)
        return pltpu.make_async_remote_copy(
            src_ref=own, dst_ref=own, send_sem=zsend.at[k, target], recv_sem=zrecv.at[k, z],
            device_id={"pert": target}, device_id_type=MESH)

    def z_arrival(k, slot):
        there = piece(k, slot, core)
        return pltpu.make_async_remote_copy(
            src_ref=there, dst_ref=there, send_sem=zsend.at[k, slot], recv_sem=zrecv.at[k, slot],
            device_id={"pert": slot}, device_id_type=MESH)

    def relay(k, slot, target):
        there = piece(k, slot, core)
        return pltpu.make_async_remote_copy(
            src_ref=there, dst_ref=there, send_sem=fsend.at[k], recv_sem=zrecv.at[k, slot],
            device_id={"pert": target}, device_id_type=MESH)

    def c_copy(k, slot):
        there = piece(k, slot, core)
        return pltpu.make_async_remote_copy(
            src_ref=there, dst_ref=there, send_sem=csend.at[k, slot], recv_sem=crecv.at[k, slot],
            device_id={"fld": other}, device_id_type=MESH)

    def c_arrival(k, slot):
        there = piece(k, slot, other)
        return pltpu.make_async_remote_copy(
            src_ref=there, dst_ref=there, send_sem=csend.at[k, slot], recv_sem=crecv.at[k, slot],
            device_id={"fld": other}, device_id_type=MESH)

    def direct(target):
        ok = z != target
        if n == 4 and target in (0, 3):
            ok = jnp.logical_and(ok, z != 3 - target)
        return ok

    for k in range(CHUNKS):
        for t in range(n):
            @pl.when(direct(t))
            def _():
                z_copy(k, t).start()
        c_copy(k, z).start()

    s_in.wait()
    zero = jnp.zeros((SUB, 128), jnp.float32)

    def relayout_in(g, i):
        for j in range(8):
            x = vin[i, pl.ds(pl.multiple_of(g * SUB, SUB), SUB), j * 128:(j + 1) * 128]
            state[pl.ds(line(0, g * SUB) + i * SUB + j, SUB, stride=wide), :] = x

    def halo(s, side):
        q = 0 if side == 0 else rows - 1
        r = phys(q)
        beyond = phys(-1 if side == 0 else rows)
        partner = near if side == 0 else far
        there = rows - 1 - beyond
        return pltpu.make_async_remote_copy(
            src_ref=state.at[pl.ds(line(s, r), wide), :],
            dst_ref=state.at[pl.ds(line(s, there), wide), :],
            send_sem=hsend.at[s, side], recv_sem=hrecv.at[s, side],
            device_id={"lat": partner}, device_id_type=MESH)

    def halo_arrival(s, side):
        beyond = phys(-1 if side == 0 else rows)
        here = state.at[pl.ds(line(s, beyond), wide), :]
        partner = near if side == 0 else far
        return pltpu.make_async_remote_copy(
            src_ref=here, dst_ref=here, send_sem=hsend.at[s, side], recv_sem=hrecv.at[s, side],
            device_id={"lat": partner}, device_id_type=MESH)

    near_group = jnp.where(even, halves - 1, 0)

    @pl.loop(0, mf)
    def _(i):
        relayout_in(near_group, i)

    @pl.when(has_near)
    def _():
        halo(0, 0).start()

    for g in range(1, halves):
        @pl.loop(0, mf)
        def _(i):
            relayout_in(jnp.where(even, halves - 1 - g, g), i)

    if nlat > 2:
        @pl.when(has_far)
        def _():
            halo(0, 1).start()

    def clear(q):
        @pl.loop(0, STEPS)
        def _(s):
            @pl.loop(0, mf)
            def _(i):
                state[pl.ds(line(s, phys(q)) + pl.multiple_of(i * SUB, SUB), SUB), :] = zero

    @pl.when(jnp.logical_not(has_near))
    def _():
        clear(-1)

    @pl.when(jnp.logical_not(has_far))
    def _():
        clear(rows)

    total = rows * nlat

    @pl.loop(0, rows)
    def _(r):
        number = jnp.full((SUB, 128), lat * rows + r, jnp.int32).astype(jnp.float32)
        cor[pl.ds(pl.multiple_of(r * SUB, SUB), SUB), :] = 0.1 * jnp.sin(
            jnp.float32(np.pi) * ((number + 0.5) / total - 0.5))

    lane = lax.broadcasted_iota(jnp.int32, (SUB, 128), 1)
    at_first, at_last = lane == 0, lane == 127

    def collect(k):
        def pass_on(slot):
            z_arrival(k, slot).wait_recv()
            c_copy(k, slot).start()
        if n == 4:
            for end, via in ((3, 2), (0, 1)):
                @pl.when(z == via)
                def _():
                    pass_on(3 - end)
                    relay(k, 3 - end, end).start()
        for slot in range(n):
            fresh = z != slot
            if n == 4 and slot in (0, 3):
                fresh = jnp.logical_and(fresh, z != (2 if slot == 0 else 1))

            @pl.when(fresh)
            def _():
                pass_on(slot)
        for slot in range(n):
            c_arrival(k, slot).wait_recv()
        for record in range(3):
            slot = owners_ref[record]
            for f in range(4):
                for rr in range(span):
                    src = ((slot * 2 + f // 2) * span + rr) * 2 + f % 2
                    dst = (record * 4 + f) * rows + first_row(k) + rr
                    rec[pl.ds(pl.multiple_of(dst * SUB, SUB), SUB), :] = (
                        gather[k][src])

    def one_row(s, r):
        earlier, weight = s // 3, (s % 3) / 3.0

        def coef(f):
            at = ((earlier * 4 + f) * rows + r) * SUB
            low = rec[pl.ds(pl.multiple_of(at, SUB), SUB), :]
            if s % 3 == 0:
                return low
            at = (((earlier + 1) * 4 + f) * rows + r) * SUB
            return (1.0 - weight) * low + weight * rec[pl.ds(pl.multiple_of(at, SUB), SUB), :]

        half_u, half_v = 0.05 * coef(0), 0.05 * coef(1)
        depth, mix = 0.05 * coef(2), 0.1 * coef(3)
        to_e, to_w, to_n, to_s = mix - half_u, mix + half_u, mix - half_v, mix + half_v
        to_c = 1.0 - 4.0 * mix
        turn = cor[pl.ds(pl.multiple_of(r * SUB, SUB), SUB), :]
        c_at, n_at, s_at, o_at = line(s, r), line(s, r + 1), line(s, r - 1), line(s + 1, r)
        for m in range(mem):
            c, nn, ss, de, base = [], [], [], [], []
            for f in range(fields):
                off = (m * fields + f) * SUB
                x = state[pl.ds(c_at + off, SUB), :]
                north = state[pl.ds(n_at + off, SUB), :]
                south = state[pl.ds(s_at + off, SUB), :]
                e = pltpu.roll(x, 127, 1)
                e = jnp.where(at_last, pltpu.roll(e, SUB - 1, 0), e)
                w = pltpu.roll(x, 1, 1)
                w = jnp.where(at_first, pltpu.roll(w, 1, 0), w)
                c.append(x)
                nn.append(north)
                ss.append(south)
                de.append(e - w)
                base.append((to_c * x + to_e * e) + (to_w * w + to_n * north) + to_s * south)
            div = de[1] + (nn[2] - ss[2])
            new = (
                base[0] - depth * div,
                base[1] - 0.05 * de[0] + turn * c[2],
                base[2] - 0.05 * (nn[0] - ss[0]) - turn * c[1],
                base[3] - 0.025 * div,
            )
            for f in range(fields):
                state[pl.ds(o_at + (m * fields + f) * SUB, SUB), :] = new[f]

    done = [0] * STEPS
    for k in range(CHUNKS):
        last = k == CHUNKS - 1
        collect(k)
        for s in range(CAPS[k] + 1):
            limit = rows if last else max((k + 1) * span - s, 0)
            start = done[s]
            if limit <= start:
                continue
            if start == 0:
                @pl.when(has_near)
                def _():
                    halo_arrival(s, 0).wait_recv()
                one_row(s, phys(0))
                if s + 1 < STEPS:
                    @pl.when(has_near)
                    def _():
                        halo(s + 1, 0).start()
                start = 1
            if limit == rows and nlat > 2:
                @pl.when(has_far)
                def _():
                    halo_arrival(s, 1).wait_recv()
            if limit > start:
                @pl.loop(start, limit)
                def _(q):
                    one_row(s, phys(q))
            if limit == rows and nlat > 2 and s + 1 < STEPS:
                @pl.when(has_far)
                def _():
                    halo(s + 1, 1).start()
            done[s] = limit

    @pl.loop(0, mf)
    def _(i):
        for g in range(halves):
            for j in range(8):
                vout[i, g * SUB:(g + 1) * SUB, j * 128:(j + 1) * 128] = (
                    state[pl.ds(line(STEPS, g * SUB) + i * SUB + j, SUB, stride=wide), :])
    s_out = pltpu.make_async_copy(vout, out_ref, out_sem)
    s_out.start()

    for k in range(CHUNKS):
        for t in range(n):
            @pl.when(direct(t))
            def _():
                z_copy(k, t).wait_send()
            c_copy(k, t).wait_send()
        if n == 4:
            for end, via in ((3, 2), (0, 1)):
                @pl.when(z == via)
                def _():
                    relay(k, 3 - end, end).wait_send()
    for s in range(STEPS):
        @pl.when(has_near)
        def _():
            halo(s, 0).wait_send()
        if nlat > 2:
            @pl.when(has_far)
            def _():
                halo(s, 1).wait_send()
    s_out.wait()


def per_device(perturb, traj_store, owners):
    n, nlat = lax.axis_size("pert"), lax.axis_size("lat")
    mem, fields, rows, lon = perturb.shape
    span = rows // CHUNKS
    f32 = jnp.float32
    dma = pltpu.SemaphoreType.DMA
    out = pl.pallas_call(
        functools.partial(kernel, n, nlat, mem, rows),
        out_shape=jax.ShapeDtypeStruct((mem * fields, rows, lon), f32),
        in_specs=[pl.BlockSpec(memory_space=pltpu.SMEM),
                  pl.BlockSpec(memory_space=pl.ANY),
                  pl.BlockSpec(memory_space=pl.ANY)],
        out_specs=pl.BlockSpec(memory_space=pl.ANY),
        scratch_shapes=[
            pltpu.VMEM((mem * fields, rows, lon), f32),
            pltpu.VMEM((2, rows, lon), f32),
            pltpu.VMEM((mem * fields, rows, lon), f32),
            pltpu.VMEM(((STEPS + 1) * (rows + 2) * mem * fields * SUB, 128), f32),
            pltpu.VMEM((3 * 4 * rows * SUB, 128), f32),
            pltpu.VMEM((rows * SUB, 128), f32),
            pltpu.VMEM((rows * 2 * SUB, 128), f32),
            *[pltpu.VMEM((n * 2 * span * 2, SUB, 128), f32) for _ in range(CHUNKS)],
            dma((2,)), dma(()),
            dma((CHUNKS, n)), dma((CHUNKS, n)), dma((CHUNKS, n)), dma((CHUNKS, n)),
            dma((CHUNKS,)), dma((STEPS, 2)), dma((STEPS, 2)),
        ],
        compiler_params=pltpu.CompilerParams(
            collective_id=0, has_side_effects=True, vmem_limit_bytes=48 * 2**20),
    )(owners, perturb.reshape(mem * fields, rows, lon), traj_store)
    return out.reshape(mem, fields, rows, lon)


def solution(mesh):
    in_specs = (
        P(("groups", "pert", "fld"), None, "lat", None),
        P(("groups", "pert"), "fld", "lat", None),
        P("groups"),
    )
    out_specs = P(("groups", "pert", "fld"), None, "lat", None)
    return jax.shard_map(
        per_device, mesh=mesh, in_specs=in_specs, out_specs=out_specs, check_vma=False
    )
```

```python
import functools

import jax
import jax.numpy as jnp
import numpy as np
from jax import lax
from jax.experimental import pallas as pl
from jax.experimental.pallas import tpu as pltpu
from jax.sharding import PartitionSpec as P

STEPS = 6
MESH = pl.DeviceIdType.MESH
SUB = 8
SPAN = 4
PAIR = 2


def chunk_plan(nlat, rows, reach):
    plan = [("far", rows, rows + reach)] if nlat > 2 else []
    plan += [("own", q, q + SPAN) for q in range(rows - SPAN, -1, -SPAN)]
    return plan + [("near", -reach, 0)]


def kernel(n, nlat, mem, rows, plan, owners_ref, perturb_ref, traj_ref, out_ref,
           vin, tin, vout, rec, cor, own, *rest):
    state, rest = rest[:STEPS + 1], rest[STEPS + 1:]
    count = len(plan)
    gather = rest[:count]
    (in_sem, out_sem, zsend, zrecv, csend, crecv, fsend,
     hsend, hrecv, bsend, brecv) = rest[count:]
    z = lax.axis_index("pert")
    core = lax.axis_index("fld")
    lat = lax.axis_index("lat")
    other = 1 - core
    even = lat % 2 == 0
    near = jnp.where(even, lat + 1, lat - 1)
    far = jnp.where(even, lat - 1, lat + 1)
    has_near = near < nlat
    has_far = jnp.logical_and(far >= 0, far < nlat)
    fields = 4
    mf = mem * fields
    wide = mf * SUB
    reach = STEPS - 1
    halves = rows // SUB
    sides = {"near": (0, near, has_near), "far": (1, far, has_far)}
    if nlat <= 2:
        del sides["far"]

    def guarded(kind):
        def run(body):
            if kind == "own":
                body()
            else:
                pl.when(sides[kind][2])(body)
        return run

    def phys(q):
        return jnp.where(even, rows - 1 - q, q)

    def line(r):
        return pl.multiple_of((r + STEPS) * wide, wide)

    def start_of(k):
        _, q0, q1 = plan[k]
        return jnp.where(even, rows - q1, q0)

    t_in = pltpu.make_async_copy(traj_ref.at[0], tin, in_sem.at[0])
    t_in.start()
    s_in = pltpu.make_async_copy(perturb_ref, vin, in_sem.at[1])
    s_in.start()

    barrier = pltpu.get_barrier_semaphore()
    for t in range(n):
        @pl.when(z != t)
        def _():
            pl.semaphore_signal(barrier, inc=1, device_id={"pert": t}, device_id_type=MESH)
    pl.semaphore_signal(barrier, inc=1, device_id={"fld": other}, device_id_type=MESH)
    amount = n - 1 + 1
    for kind, (_, partner, present) in sides.items():
        @pl.when(present)
        def _():
            pl.semaphore_signal(barrier, inc=1, device_id={"lat": partner}, device_id_type=MESH)
        amount = amount + jnp.where(present, 1, 0)

    def piece(k, slot, half):
        block = (plan[k][2] - plan[k][1]) * 2
        return gather[k].at[pl.ds((slot * 2 + half) * block, block)]

    t_in.wait()
    for f in range(2):
        for g in range(halves):
            for j in range(8):
                own[pl.ds((g * SUB * 2 + f) * SUB + j, SUB, stride=2 * SUB), :] = (
                    tin[f, g * SUB:(g + 1) * SUB, j * 128:(j + 1) * 128])
    whole = own.reshape(rows * 2, SUB, 128)
    for k, (kind, q0, q1) in enumerate(plan):
        if kind != "own":
            continue
        block = (q1 - q0) * 2
        for i in range(block):
            src = pl.multiple_of((start_of(k) * 2 + i) * SUB, SUB)
            gather[k][(z * 2 + core) * block + i] = own[pl.ds(src, SUB), :]

    pl.semaphore_wait(barrier, amount)

    def border(kind, k):
        side, partner, _ = sides[kind]
        src = jnp.where(partner > lat, rows - reach, 0)
        return pltpu.make_async_remote_copy(
            src_ref=whole.at[pl.ds(src * 2, reach * 2)], dst_ref=piece(k, z, core),
            send_sem=bsend.at[side], recv_sem=brecv.at[side],
            device_id={"lat": partner}, device_id_type=MESH)

    def z_copy(k, target):
        mine = piece(k, z, core)
        return pltpu.make_async_remote_copy(
            src_ref=mine, dst_ref=mine, send_sem=zsend.at[k, target], recv_sem=zrecv.at[k, z],
            device_id={"pert": target}, device_id_type=MESH)

    def z_arrival(k, slot):
        there = piece(k, slot, core)
        return pltpu.make_async_remote_copy(
            src_ref=there, dst_ref=there, send_sem=zsend.at[k, slot], recv_sem=zrecv.at[k, slot],
            device_id={"pert": slot}, device_id_type=MESH)

    def relay(k, slot, target):
        there = piece(k, slot, core)
        return pltpu.make_async_remote_copy(
            src_ref=there, dst_ref=there, send_sem=fsend.at[k], recv_sem=zrecv.at[k, slot],
            device_id={"pert": target}, device_id_type=MESH)

    def c_copy(k, slot):
        there = piece(k, slot, core)
        return pltpu.make_async_remote_copy(
            src_ref=there, dst_ref=there, send_sem=csend.at[k, slot], recv_sem=crecv.at[k, slot],
            device_id={"fld": other}, device_id_type=MESH)

    def c_arrival(k, slot):
        there = piece(k, slot, other)
        return pltpu.make_async_remote_copy(
            src_ref=there, dst_ref=there, send_sem=csend.at[k, slot], recv_sem=crecv.at[k, slot],
            device_id={"fld": other}, device_id_type=MESH)

    def direct(target):
        ok = z != target
        if n == 4 and target in (0, 3):
            ok = jnp.logical_and(ok, z != 3 - target)
        return ok

    def send_out(k):
        for t in range(n):
            @pl.when(direct(t))
            def _():
                z_copy(k, t).start()
        c_copy(k, z).start()

    for k, (kind, _, _) in enumerate(plan):
        if kind != "own":
            @guarded(kind)
            def _():
                border(kind, k).start()
    for k, (kind, _, _) in enumerate(plan):
        if kind == "own":
            send_out(k)

    s_in.wait()
    zero = jnp.zeros((SUB, 128), jnp.float32)

    @pl.loop(0, mf)
    def _(i):
        for g in range(halves):
            for j in range(8):
                x = vin[i, g * SUB:(g + 1) * SUB, j * 128:(j + 1) * 128]
                state[0][pl.ds(line(g * SUB) + i * SUB + j, SUB, stride=wide), :] = x

    def halo(kind):
        side, partner, _ = sides[kind]
        src = jnp.where(partner > lat, rows - STEPS, 0)
        dst = jnp.where(partner > lat, -STEPS, rows)
        return pltpu.make_async_remote_copy(
            src_ref=state[0].at[pl.ds(line(src), STEPS * wide), :],
            dst_ref=state[0].at[pl.ds(line(dst), STEPS * wide), :],
            send_sem=hsend.at[side], recv_sem=hrecv.at[side],
            device_id={"lat": partner}, device_id_type=MESH)

    def halo_arrival(kind):
        side, partner, _ = sides[kind]
        here = state[0].at[pl.ds(line(jnp.where(partner > lat, rows, -STEPS)), STEPS * wide), :]
        return pltpu.make_async_remote_copy(
            src_ref=here, dst_ref=here, send_sem=hsend.at[side], recv_sem=hrecv.at[side],
            device_id={"lat": partner}, device_id_type=MESH)

    for k, (kind, _, _) in enumerate(plan):
        if kind != "own":
            @guarded(kind)
            def _():
                halo(kind).start()
                border(kind, k).wait_recv()
                send_out(k)

    def clear(q):
        for s in range(STEPS):
            @pl.loop(0, mf)
            def _(i):
                state[s][pl.ds(line(phys(q)) + pl.multiple_of(i * SUB, SUB), SUB), :] = zero

    @pl.when(jnp.logical_not(has_near))
    def _():
        clear(-1)

    @pl.when(jnp.logical_not(has_far))
    def _():
        clear(rows)

    total = rows * nlat

    @pl.loop(0, rows + 2 * reach)
    def _(r):
        number = jnp.full((SUB, 128), lat * rows + r - reach, jnp.int32).astype(jnp.float32)
        cor[r] = 0.1 * jnp.sin(jnp.float32(np.pi) * ((number + 0.5) / total - 0.5))

    lane = lax.broadcasted_iota(jnp.int32, (SUB, 128), 1)
    at_first, at_last = lane == 0, lane == 127

    def collect(k):
        span = plan[k][2] - plan[k][1]

        def pass_on(slot):
            z_arrival(k, slot).wait_recv()
            c_copy(k, slot).start()
        if n == 4:
            for end, via in ((3, 2), (0, 1)):
                @pl.when(z == via)
                def _():
                    z_arrival(k, 3 - end).wait_recv()
                    relay(k, 3 - end, end).start()
                    c_copy(k, 3 - end).start()
        for slot in range(n):
            fresh = z != slot
            if n == 4 and slot in (0, 3):
                fresh = jnp.logical_and(fresh, z != (2 if slot == 0 else 1))

            @pl.when(fresh)
            def _():
                pass_on(slot)
        for slot in range(n):
            c_arrival(k, slot).wait_recv()
        for record in range(3):
            slot = owners_ref[record]
            for f in range(4):
                for rr in range(span):
                    src = ((slot * 2 + f // 2) * span + rr) * 2 + f % 2
                    rec[(start_of(k) + rr + reach) * 12 + record * 4 + f] = gather[k][src]

    def one_row(s, r):
        earlier, weight = s // 3, (s % 3) / 3.0

        def coef(f):
            at = (r + reach) * 12 + earlier * 4 + f
            low = rec[at]
            if s % 3 == 0:
                return low
            return (1.0 - weight) * low + weight * rec[at + 4]

        half_u, half_v = 0.05 * coef(0), 0.05 * coef(1)
        depth, mix = 0.05 * coef(2), 0.1 * coef(3)
        to_e, to_w, to_n, to_s = mix - half_u, mix + half_u, mix - half_v, mix + half_v
        to_c = 1.0 - 4.0 * mix
        turn = cor[r + reach]
        c_at, n_at, s_at = line(r), line(r + 1), line(r - 1)
        held = []

        def flush():
            for at, value in held:
                state[s + 1][pl.ds(at, SUB), :] = value
            held.clear()

        for m in range(mem):
            c, nn, ss, de, base = [], [], [], [], []
            for f in range(fields):
                off = (m * fields + f) * SUB
                x = state[s][pl.ds(c_at + off, SUB), :]
                north = state[s][pl.ds(n_at + off, SUB), :]
                south = state[s][pl.ds(s_at + off, SUB), :]
                e = pltpu.roll(x, 127, 1)
                e = jnp.where(at_last, pltpu.roll(e, SUB - 1, 0), e)
                w = pltpu.roll(x, 1, 1)
                w = jnp.where(at_first, pltpu.roll(w, 1, 0), w)
                c.append(x)
                nn.append(north)
                ss.append(south)
                de.append(e - w)
                base.append((to_c * x + to_e * e) + (to_w * w + to_n * north) + to_s * south)
            div = de[1] + (nn[2] - ss[2])
            new = (
                base[0] - depth * div,
                base[1] - 0.05 * de[0] + turn * c[2],
                base[2] - 0.05 * (nn[0] - ss[0]) - turn * c[1],
                base[3] - 0.025 * div,
            )
            flush()
            held += [(c_at + (m * fields + f) * SUB, new[f]) for f in range(fields)]
        flush()

    def rows_of(s, low, high):
        if isinstance(low, int) and isinstance(high, int):
            pairs = max(high - low, 0) // PAIR
            if pairs:
                @pl.loop(0, pairs)
                def _(p):
                    for i in range(PAIR):
                        one_row(s, phys(low + p * PAIR + i))
            for q in range(low + pairs * PAIR, high):
                one_row(s, phys(q))
        else:
            @pl.loop(low, high)
            def _(q):
                one_row(s, phys(q))

    done = [rows + (jnp.where(has_far, reach - s, 0) if nlat > 2 else 0) for s in range(STEPS)]
    for k, (kind, front, _) in enumerate(plan):
        @guarded(kind)
        def _():
            collect(k)
        if kind == "far":
            @guarded(kind)
            def _():
                halo_arrival(kind).wait_recv()
            continue
        if front == 0:
            @guarded("near")
            def _():
                halo_arrival("near").wait_recv()
        for s in range(STEPS):
            low = front + s
            if kind == "near" and nlat % 2:
                low = jnp.where(has_near, low, 0)
            elif low >= rows:
                continue
            rows_of(s, low, done[s])
            done[s] = low

    @pl.loop(0, mf)
    def _(i):
        for g in range(halves):
            for j in range(8):
                vout[i, g * SUB:(g + 1) * SUB, j * 128:(j + 1) * 128] = (
                    state[STEPS][pl.ds(line(g * SUB) + i * SUB + j, SUB, stride=wide), :])
    s_out = pltpu.make_async_copy(vout, out_ref, out_sem)
    s_out.start()

    for k, (kind, _, _) in enumerate(plan):
        @guarded(kind)
        def _():
            for t in range(n):
                @pl.when(direct(t))
                def _():
                    z_copy(k, t).wait_send()
                c_copy(k, t).wait_send()
            if n == 4:
                for end, via in ((3, 2), (0, 1)):
                    @pl.when(z == via)
                    def _():
                        relay(k, 3 - end, end).wait_send()
            if kind != "own":
                border(kind, k).wait_send()
                halo(kind).wait_send()
    s_out.wait()


def per_device(perturb, traj_store, owners):
    n, nlat = lax.axis_size("pert"), lax.axis_size("lat")
    mem, fields, rows, lon = perturb.shape
    reach = STEPS - 1
    plan = chunk_plan(nlat, rows, reach)
    f32 = jnp.float32
    dma = pltpu.SemaphoreType.DMA
    marks = dma((len(plan), n))
    out = pl.pallas_call(
        functools.partial(kernel, n, nlat, mem, rows, plan),
        out_shape=jax.ShapeDtypeStruct((mem * fields, rows, lon), f32),
        in_specs=[pl.BlockSpec(memory_space=pltpu.SMEM),
                  pl.BlockSpec(memory_space=pl.ANY),
                  pl.BlockSpec(memory_space=pl.ANY)],
        out_specs=pl.BlockSpec(memory_space=pl.ANY),
        scratch_shapes=[
            pltpu.VMEM((mem * fields, rows, lon), f32),
            pltpu.VMEM((2, rows, lon), f32),
            pltpu.VMEM((mem * fields, rows, lon), f32),
            pltpu.VMEM(((rows + 2 * reach) * 12, SUB, 128), f32),
            pltpu.VMEM((rows + 2 * reach, SUB, 128), f32),
            pltpu.VMEM((rows * 2 * SUB, 128), f32),
            *[pltpu.VMEM(((rows + 2 * STEPS) * mem * fields * SUB, 128), f32)
              for _ in range(STEPS + 1)],
            *[pltpu.VMEM((n * 2 * (q1 - q0) * 2, SUB, 128), f32) for _, q0, q1 in plan],
            dma((2,)), dma(()), marks, marks, marks, marks, dma((len(plan),)),
            dma((2,)), dma((2,)), dma((2,)), dma((2,)),
        ],
        compiler_params=pltpu.CompilerParams(
            collective_id=0, has_side_effects=True, vmem_limit_bytes=48 * 2**20),
    )(owners, perturb.reshape(mem * fields, rows, lon), traj_store)
    return out.reshape(mem, fields, rows, lon)


def solution(mesh):
    in_specs = (
        P(("groups", "pert", "fld"), None, "lat", None),
        P(("groups", "pert"), "fld", "lat", None),
        P("groups"),
    )
    out_specs = P(("groups", "pert", "fld"), None, "lat", None)
    return jax.shard_map(
        per_device, mesh=mesh, in_specs=in_specs, out_specs=out_specs, check_vma=False
    )
```

```python
import functools

import jax
import jax.numpy as jnp
import numpy as np
from jax import lax
from jax.experimental import pallas as pl
from jax.experimental.pallas import tpu as pltpu
from jax.sharding import PartitionSpec as P

STEPS = 6
MESH = pl.DeviceIdType.MESH
SUB = 8
SPAN = 8
PAIR = 4


def chunk_plan(nlat, rows, reach):
    plan = [("far", rows, rows + reach)] if nlat > 2 else []
    plan += [("own", q, q + SPAN) for q in range(rows - SPAN, -1, -SPAN)]
    return plan + [("near", -reach, 0)]


def kernel(n, nlat, mem, rows, plan, owners_ref, perturb_ref, traj_ref, out_ref,
           vin, tin, vout, rec, cor, own, *rest):
    state, rest = rest[:STEPS + 1], rest[STEPS + 1:]
    count = len(plan)
    gather = rest[:count]
    (in_sem, out_sem, zsend, zrecv, csend, crecv, fsend,
     hsend, hrecv, bsend, brecv) = rest[count:]
    z = lax.axis_index("pert")
    core = lax.axis_index("fld")
    lat = lax.axis_index("lat")
    other = 1 - core
    even = lat % 2 == 0
    near = jnp.where(even, lat + 1, lat - 1)
    far = jnp.where(even, lat - 1, lat + 1)
    has_near = near < nlat
    has_far = jnp.logical_and(far >= 0, far < nlat)
    fields = 4
    mf = mem * fields
    wide = mf * SUB
    reach = STEPS - 1
    halves = rows // SUB
    sides = {"near": (0, near, has_near), "far": (1, far, has_far)}
    if nlat <= 2:
        del sides["far"]

    def guarded(kind):
        def run(body):
            if kind == "own":
                body()
            else:
                pl.when(sides[kind][2])(body)
        return run

    def phys(q):
        return jnp.where(even, rows - 1 - q, q)

    def line(r):
        return pl.multiple_of((r + STEPS) * wide, wide)

    def start_of(k):
        _, q0, q1 = plan[k]
        return jnp.where(even, rows - q1, q0)

    t_in = pltpu.make_async_copy(traj_ref.at[0], tin, in_sem.at[0])
    t_in.start()
    s_in = pltpu.make_async_copy(perturb_ref, vin, in_sem.at[1])
    s_in.start()

    barrier = pltpu.get_barrier_semaphore()
    for t in range(n):
        @pl.when(z != t)
        def _():
            pl.semaphore_signal(barrier, inc=1, device_id={"pert": t}, device_id_type=MESH)
    pl.semaphore_signal(barrier, inc=1, device_id={"fld": other}, device_id_type=MESH)
    amount = n - 1 + 1
    for kind, (_, partner, present) in sides.items():
        @pl.when(present)
        def _():
            pl.semaphore_signal(barrier, inc=1, device_id={"lat": partner}, device_id_type=MESH)
        amount = amount + jnp.where(present, 1, 0)

    def piece(k, slot, half):
        block = (plan[k][2] - plan[k][1]) * 2
        return gather[k].at[pl.ds((slot * 2 + half) * block, block)]

    t_in.wait()
    for f in range(2):
        for g in range(halves):
            for j in range(8):
                own[pl.ds((g * SUB * 2 + f) * SUB + j, SUB, stride=2 * SUB), :] = (
                    tin[f, g * SUB:(g + 1) * SUB, j * 128:(j + 1) * 128])
    whole = own.reshape(rows * 2, SUB, 128)
    for k, (kind, q0, q1) in enumerate(plan):
        if kind != "own":
            continue
        block = (q1 - q0) * 2
        for i in range(block):
            src = pl.multiple_of((start_of(k) * 2 + i) * SUB, SUB)
            gather[k][(z * 2 + core) * block + i] = own[pl.ds(src, SUB), :]

    pl.semaphore_wait(barrier, amount)

    def border(kind, k):
        side, partner, _ = sides[kind]
        src = jnp.where(partner > lat, rows - reach, 0)
        return pltpu.make_async_remote_copy(
            src_ref=whole.at[pl.ds(src * 2, reach * 2)], dst_ref=piece(k, z, core),
            send_sem=bsend.at[side], recv_sem=brecv.at[side],
            device_id={"lat": partner}, device_id_type=MESH)

    def z_copy(k, target):
        mine = piece(k, z, core)
        return pltpu.make_async_remote_copy(
            src_ref=mine, dst_ref=mine, send_sem=zsend.at[k, target], recv_sem=zrecv.at[k, z],
            device_id={"pert": target}, device_id_type=MESH)

    def z_arrival(k, slot):
        there = piece(k, slot, core)
        return pltpu.make_async_remote_copy(
            src_ref=there, dst_ref=there, send_sem=zsend.at[k, slot], recv_sem=zrecv.at[k, slot],
            device_id={"pert": slot}, device_id_type=MESH)

    def relay(k, slot, target):
        there = piece(k, slot, core)
        return pltpu.make_async_remote_copy(
            src_ref=there, dst_ref=there, send_sem=fsend.at[k], recv_sem=zrecv.at[k, slot],
            device_id={"pert": target}, device_id_type=MESH)

    def c_copy(k, slot):
        there = piece(k, slot, core)
        return pltpu.make_async_remote_copy(
            src_ref=there, dst_ref=there, send_sem=csend.at[k, slot], recv_sem=crecv.at[k, slot],
            device_id={"fld": other}, device_id_type=MESH)

    def c_arrival(k, slot):
        there = piece(k, slot, other)
        return pltpu.make_async_remote_copy(
            src_ref=there, dst_ref=there, send_sem=csend.at[k, slot], recv_sem=crecv.at[k, slot],
            device_id={"fld": other}, device_id_type=MESH)

    def direct(target):
        ok = z != target
        if n == 4 and target in (0, 3):
            ok = jnp.logical_and(ok, z != 3 - target)
        return ok

    def send_out(k):
        for t in range(n):
            @pl.when(direct(t))
            def _():
                z_copy(k, t).start()
        c_copy(k, z).start()

    for k, (kind, _, _) in enumerate(plan):
        if kind != "own":
            @guarded(kind)
            def _():
                border(kind, k).start()
    for k, (kind, _, _) in enumerate(plan):
        if kind == "own":
            send_out(k)

    s_in.wait()
    zero = jnp.zeros((SUB, 128), jnp.float32)

    @pl.loop(0, mf)
    def _(i):
        for g in range(halves):
            for j in range(8):
                x = vin[i, g * SUB:(g + 1) * SUB, j * 128:(j + 1) * 128]
                state[0][pl.ds(line(g * SUB) + i * SUB + j, SUB, stride=wide), :] = x

    def halo(kind):
        side, partner, _ = sides[kind]
        src = jnp.where(partner > lat, rows - STEPS, 0)
        dst = jnp.where(partner > lat, -STEPS, rows)
        return pltpu.make_async_remote_copy(
            src_ref=state[0].at[pl.ds(line(src), STEPS * wide), :],
            dst_ref=state[0].at[pl.ds(line(dst), STEPS * wide), :],
            send_sem=hsend.at[side], recv_sem=hrecv.at[side],
            device_id={"lat": partner}, device_id_type=MESH)

    def halo_arrival(kind):
        side, partner, _ = sides[kind]
        here = state[0].at[pl.ds(line(jnp.where(partner > lat, rows, -STEPS)), STEPS * wide), :]
        return pltpu.make_async_remote_copy(
            src_ref=here, dst_ref=here, send_sem=hsend.at[side], recv_sem=hrecv.at[side],
            device_id={"lat": partner}, device_id_type=MESH)

    for k, (kind, _, _) in enumerate(plan):
        if kind != "own":
            @guarded(kind)
            def _():
                halo(kind).start()
                border(kind, k).wait_recv()
                send_out(k)

    def clear(q):
        for s in range(STEPS):
            @pl.loop(0, mf)
            def _(i):
                state[s][pl.ds(line(phys(q)) + pl.multiple_of(i * SUB, SUB), SUB), :] = zero

    @pl.when(jnp.logical_not(has_near))
    def _():
        clear(-1)

    @pl.when(jnp.logical_not(has_far))
    def _():
        clear(rows)

    total = rows * nlat

    @pl.loop(0, rows + 2 * reach)
    def _(r):
        number = jnp.full((SUB, 128), lat * rows + r - reach, jnp.int32).astype(jnp.float32)
        cor[r] = 0.1 * jnp.sin(jnp.float32(np.pi) * ((number + 0.5) / total - 0.5))

    lane = lax.broadcasted_iota(jnp.int32, (SUB, 128), 1)
    at_first, at_last = lane == 0, lane == 127

    def collect(k):
        span = plan[k][2] - plan[k][1]

        def pass_on(slot):
            z_arrival(k, slot).wait_recv()
            c_copy(k, slot).start()
        if n == 4:
            for end, via in ((3, 2), (0, 1)):
                @pl.when(z == via)
                def _():
                    z_arrival(k, 3 - end).wait_recv()
                    relay(k, 3 - end, end).start()
                    c_copy(k, 3 - end).start()
        for slot in range(n):
            fresh = z != slot
            if n == 4 and slot in (0, 3):
                fresh = jnp.logical_and(fresh, z != (2 if slot == 0 else 1))

            @pl.when(fresh)
            def _():
                pass_on(slot)
        for slot in range(n):
            c_arrival(k, slot).wait_recv()
        for record in range(3):
            slot = owners_ref[record]
            for f in range(4):
                for rr in range(span):
                    src = ((slot * 2 + f // 2) * span + rr) * 2 + f % 2
                    rec[(start_of(k) + rr + reach) * 12 + record * 4 + f] = gather[k][src]

    def one_row(s, r):
        earlier, weight = s // 3, (s % 3) / 3.0

        def coef(f):
            at = (r + reach) * 12 + earlier * 4 + f
            low = rec[at]
            if s % 3 == 0:
                return low
            return (1.0 - weight) * low + weight * rec[at + 4]

        half_u, half_v = 0.05 * coef(0), 0.05 * coef(1)
        depth, mix = 0.05 * coef(2), 0.1 * coef(3)
        to_e, to_w, to_n, to_s = mix - half_u, mix + half_u, mix - half_v, mix + half_v
        to_c = 1.0 - 4.0 * mix
        turn = cor[r + reach]
        c_at, n_at, s_at = line(r), line(r + 1), line(r - 1)
        held = []

        def flush():
            for at, value in held:
                state[s + 1][pl.ds(at, SUB), :] = value
            held.clear()

        for m in range(mem):
            c, nn, ss, de, base = [], [], [], [], []
            for f in range(fields):
                off = (m * fields + f) * SUB
                x = state[s][pl.ds(c_at + off, SUB), :]
                north = state[s][pl.ds(n_at + off, SUB), :]
                south = state[s][pl.ds(s_at + off, SUB), :]
                e = pltpu.roll(x, 127, 1)
                e = jnp.where(at_last, pltpu.roll(e, SUB - 1, 0), e)
                w = pltpu.roll(x, 1, 1)
                w = jnp.where(at_first, pltpu.roll(w, 1, 0), w)
                c.append(x)
                nn.append(north)
                ss.append(south)
                de.append(e - w)
                base.append((to_c * x + to_e * e) + (to_w * w + to_n * north) + to_s * south)
            div = de[1] + (nn[2] - ss[2])
            new = (
                base[0] - depth * div,
                base[1] - 0.05 * de[0] + turn * c[2],
                base[2] - 0.05 * (nn[0] - ss[0]) - turn * c[1],
                base[3] - 0.025 * div,
            )
            flush()
            held += [(c_at + (m * fields + f) * SUB, new[f]) for f in range(fields)]
        flush()

    def rows_of(s, low, high):
        if isinstance(low, int) and isinstance(high, int):
            pairs = max(high - low, 0) // PAIR
            if pairs:
                @pl.loop(0, pairs)
                def _(p):
                    for i in range(PAIR):
                        one_row(s, phys(low + p * PAIR + i))
            for q in range(low + pairs * PAIR, high):
                one_row(s, phys(q))
        else:
            @pl.loop(low, high)
            def _(q):
                one_row(s, phys(q))

    done = [rows + (jnp.where(has_far, reach - s, 0) if nlat > 2 else 0) for s in range(STEPS)]
    for k, (kind, front, _) in enumerate(plan):
        @guarded(kind)
        def _():
            collect(k)
        if kind == "far":
            @guarded(kind)
            def _():
                halo_arrival(kind).wait_recv()
            continue
        if front == 0:
            @guarded("near")
            def _():
                halo_arrival("near").wait_recv()
        for s in range(STEPS):
            low = front + s
            if kind == "near" and nlat % 2:
                low = jnp.where(has_near, low, 0)
            elif low >= rows:
                continue
            rows_of(s, low, done[s])
            done[s] = low

    @pl.loop(0, mf)
    def _(i):
        for g in range(halves):
            for j in range(8):
                vout[i, g * SUB:(g + 1) * SUB, j * 128:(j + 1) * 128] = (
                    state[STEPS][pl.ds(line(g * SUB) + i * SUB + j, SUB, stride=wide), :])
    s_out = pltpu.make_async_copy(vout, out_ref, out_sem)
    s_out.start()

    for k, (kind, _, _) in enumerate(plan):
        @guarded(kind)
        def _():
            for t in range(n):
                @pl.when(direct(t))
                def _():
                    z_copy(k, t).wait_send()
                c_copy(k, t).wait_send()
            if n == 4:
                for end, via in ((3, 2), (0, 1)):
                    @pl.when(z == via)
                    def _():
                        relay(k, 3 - end, end).wait_send()
            if kind != "own":
                border(kind, k).wait_send()
                halo(kind).wait_send()
    s_out.wait()


def per_device(perturb, traj_store, owners):
    n, nlat = lax.axis_size("pert"), lax.axis_size("lat")
    mem, fields, rows, lon = perturb.shape
    reach = STEPS - 1
    plan = chunk_plan(nlat, rows, reach)
    f32 = jnp.float32
    dma = pltpu.SemaphoreType.DMA
    marks = dma((len(plan), n))
    out = pl.pallas_call(
        functools.partial(kernel, n, nlat, mem, rows, plan),
        out_shape=jax.ShapeDtypeStruct((mem * fields, rows, lon), f32),
        in_specs=[pl.BlockSpec(memory_space=pltpu.SMEM),
                  pl.BlockSpec(memory_space=pl.ANY),
                  pl.BlockSpec(memory_space=pl.ANY)],
        out_specs=pl.BlockSpec(memory_space=pl.ANY),
        scratch_shapes=[
            pltpu.VMEM((mem * fields, rows, lon), f32),
            pltpu.VMEM((2, rows, lon), f32),
            pltpu.VMEM((mem * fields, rows, lon), f32),
            pltpu.VMEM(((rows + 2 * reach) * 12, SUB, 128), f32),
            pltpu.VMEM((rows + 2 * reach, SUB, 128), f32),
            pltpu.VMEM((rows * 2 * SUB, 128), f32),
            *[pltpu.VMEM(((rows + 2 * STEPS) * mem * fields * SUB, 128), f32)
              for _ in range(STEPS + 1)],
            *[pltpu.VMEM((n * 2 * (q1 - q0) * 2, SUB, 128), f32) for _, q0, q1 in plan],
            dma((2,)), dma(()), marks, marks, marks, marks, dma((len(plan),)),
            dma((2,)), dma((2,)), dma((2,)), dma((2,)),
        ],
        compiler_params=pltpu.CompilerParams(
            collective_id=0, has_side_effects=True, vmem_limit_bytes=60 * 2**20),
    )(owners, perturb.reshape(mem * fields, rows, lon), traj_store)
    return out.reshape(mem, fields, rows, lon)


def solution(mesh):
    in_specs = (
        P(("groups", "pert", "fld"), None, "lat", None),
        P(("groups", "pert"), "fld", "lat", None),
        P("groups"),
    )
    out_specs = P(("groups", "pert", "fld"), None, "lat", None)
    return jax.shard_map(
        per_device, mesh=mesh, in_specs=in_specs, out_specs=out_specs, check_vma=False
    )
```
